32 devices in a mesh: dom: 16 (over z, y, x), band: 2 (over core).
Axes of the slice: x: 2, y: 2, z: 4, core: 2. Of those that a mesh axis runs over, the one named last changes fastest.
Arguments:
- vectors: bfloat16 [8192, 768], P('dom', 'band'), may hold values from -16 to 16
- cell_ham: bfloat16 [8, 512, 512], replicated, may hold values from -0.25 to 0.25
- cell_type: int32 [32], P('dom'), may hold values from 0 to 7
- cell_nodes: int32 [32, 512], P('dom'), may hold values from 0 to 767, as said below
- shared_nodes: int32 [16, 256], P('dom'), may hold values from 0 to 511, as said below
Outputs:
- filtered: bfloat16 [8192, 768], P('dom', 'band')
- margin: float32 [2, 384, 768], P('band', 'dom')
The draws below stay inside these ranges and needn't reach their ends.
Inputs may be any that keep to these rules, and one draw needn't show every extreme that they name: `cell_nodes`: the 512 entries of each cell are distinct. `shared_nodes`: the 256 entries of each row are distinct.
All inputs are finite; a program needn't handle non-finite values.
Results may differ from the reference program's by a relative error of at most 0.0045.
Values may be sent and summed in bfloat16 or wider, within the bound.
A program may use at most 64 MiB of HBM per device.

```python
import jax
import jax.numpy as jnp
from jax import lax

CN = 512
BAND_DEV = 384
NTYPES = 8
GHOST = 128
NODES_DEV = 512
CELLS_DEV = 2
BANDS = 768
NODES = 8192
CELLS = 32
N_DOM = 16
N_BAND = 2


def pick_distinct(subkey, extent, chosen_count, leading_cell):
    scores = jax.random.permutation(subkey, extent).astype(jnp.int32)
    positions = jnp.arange(extent, dtype=jnp.int32)
    forced = jnp.where(leading_cell & (positions == 0), -2, jnp.where(leading_cell & (positions == extent - 1), -1, scores))
    ranked = jnp.argsort(forced, stable=True)
    picked = ranked[:chosen_count]
    return jax.random.permutation(jax.random.fold_in(subkey, 7), picked).astype(jnp.int32)


def draw_cell_nodes(key, part):
    extent = NODES_DEV + 2 * GHOST
    subkeys = jax.random.split(jax.random.fold_in(key, 11), CELLS)
    leading_cell = jnp.arange(CELLS) % CELLS_DEV == 0
    return jax.vmap(lambda subkey, leading: pick_distinct(subkey, extent, CN, leading))(subkeys, leading_cell).astype(jnp.int32)


def draw_shared_nodes(key, part):
    subkeys = jax.random.split(jax.random.fold_in(key, 13), N_DOM)
    leading_cell = jnp.ones((N_DOM,), dtype=bool)
    return jax.vmap(lambda subkey, leading: pick_distinct(subkey, NODES_DEV, 2 * GHOST, leading))(subkeys, leading_cell).astype(jnp.int32)


def draw_vectors(key, part):
    key_common, key_weight, key_noise = jax.random.split(jax.random.fold_in(key, 17), 3)
    key_pairing = jax.random.fold_in(key, 19)
    common = jax.random.normal(key_common, (NODES, 1), jnp.float32)
    weights = jax.random.normal(key_weight, (1, BANDS), jnp.float32)
    pairing = jax.random.permutation(key_pairing, N_DOM).astype(jnp.int32)
    node_domain = (jnp.arange(NODES, dtype=jnp.int32) // NODES_DEV).astype(jnp.int32)
    target_domain = pairing[node_domain]
    column_owner = (jnp.arange(BANDS, dtype=jnp.int32) % BAND_DEV // (BAND_DEV // N_DOM)).astype(jnp.int32)
    heavy = jnp.where(target_domain[:, None] == column_owner[None, :], 5.0, 1.0).astype(jnp.float32)
    noise = jax.random.normal(key_noise, (NODES, BANDS), jnp.float32)
    values = 0.7 * common * weights + 0.7 * noise
    return jnp.clip(values * heavy, -16.0, 16.0).astype(jnp.bfloat16)


def place_ends(drawn, key, low, high):
    spot = [jax.random.randint(jax.random.fold_in(key, axis), (), 0, length) for axis, length in enumerate(drawn.shape)]
    widest = drawn.shape.index(max(drawn.shape))
    next_to = spot[:widest] + [(spot[widest] + 1) % drawn.shape[widest]] + spot[widest + 1:]
    return drawn.at[tuple(spot)].set(low).at[tuple(next_to)].set(high)


def normal_values(stream_key, shape, scale, limit, kind=jnp.bfloat16):
    drawn = jax.random.normal(stream_key, shape, jnp.float32) * scale
    return jnp.minimum(jnp.maximum(drawn, -limit), limit).astype(kind)


def setup_inputs(seed: int = 0) -> dict:
    key_of = jax.random.split(jax.random.key(seed), 6)
    vectors = draw_vectors(jax.random.fold_in(key_of[5], 71), 0)
    cell_ham = normal_values(key_of[1], (NTYPES, CN, CN), CN ** -0.5, 0.25)
    cell_type = place_ends(jax.random.randint(key_of[2], (CELLS,), 0, NTYPES), jax.random.fold_in(key_of[2], 1), 0, NTYPES - 1).astype(jnp.int32)
    cell_nodes = draw_cell_nodes(jax.random.fold_in(key_of[5], 71), 0)
    shared_nodes = draw_shared_nodes(jax.random.fold_in(key_of[5], 71), 0)
    return dict(vectors=vectors, cell_ham=cell_ham, cell_type=cell_type, cell_nodes=cell_nodes, shared_nodes=shared_nodes)


SHIFT = 0.5
INV_HALF = 0.5


def extended_map(shared_nodes):
    domains = jnp.arange(N_DOM, dtype=jnp.int32)[:, None]
    absent = N_DOM * NODES_DEV
    preceding = jnp.roll(shared_nodes, 1, axis=0)[:, GHOST:]
    following = jnp.roll(shared_nodes, -1, axis=0)[:, :GHOST]
    lower_rim = jnp.where(domains > 0, (domains - 1) * NODES_DEV + preceding, absent)
    owned_rows = domains * NODES_DEV + jnp.arange(NODES_DEV, dtype=jnp.int32)[None, :]
    upper_rim = jnp.where(domains < N_DOM - 1, (domains + 1) * NODES_DEV + following, absent)
    return jnp.concatenate([lower_rim, owned_rows, upper_rim], axis=1).astype(jnp.int32)


def reference(vectors, cell_ham, cell_type, cell_nodes, shared_nodes):
    node_map = extended_map(shared_nodes)
    cell_domain = (jnp.arange(CELLS, dtype=jnp.int32) // CELLS_DEV).astype(jnp.int32)
    global_cells = node_map[cell_domain[:, None], cell_nodes].astype(jnp.int32)

    def apply_operator(field):
        padded = jnp.concatenate([field, jnp.zeros((1, field.shape[1]), field.dtype)], axis=0)

        def add_cell(accumulated, cell_item):
            node_index, cell_kind = cell_item
            cell_out = jnp.dot(cell_ham[cell_kind], padded[node_index], preferred_element_type=jnp.float32)
            return accumulated.at[node_index].add(cell_out), None

        initial = jnp.zeros((NODES + 1, BANDS), jnp.float32)
        accumulated, _ = lax.scan(add_cell, initial, (global_cells, cell_type))
        return accumulated[:-1]

    initial_f = vectors.astype(jnp.float32)
    first_section = ((apply_operator(vectors) - SHIFT * initial_f) * INV_HALF).astype(jnp.bfloat16)
    second = apply_operator(first_section)
    filtered = (2.0 * (second - SHIFT * first_section.astype(jnp.float32)) * INV_HALF - initial_f).astype(jnp.bfloat16)
    margin = jnp.dot(filtered.T, filtered, preferred_element_type=jnp.float32) * (1.0 / NODES)
    return filtered, margin.reshape(N_BAND, BAND_DEV, BANDS)
```

```python
import functools

import jax
import jax.numpy as jnp
from jax import lax
from jax.experimental import pallas as pl
from jax.experimental.pallas import tpu as pltpu
from jax.sharding import PartitionSpec as P

SHIFT = 0.5
INV_HALF = 0.5
MESH = pl.DeviceIdType.MESH
F32 = jnp.float32
BF16 = jnp.bfloat16


def dot(a, b):
    return jnp.dot(a, b, preferred_element_type=F32)


def dot_tn(a, b):
    return lax.dot_general(a, b, (((0,), (0,)), ((), ())), preferred_element_type=F32)


def dot_nt(a, b):
    return lax.dot_general(a, b, (((1,), (1,)), ((), ())), preferred_element_type=F32)


def one_hot(rows, index_row):
    spots = lax.broadcasted_iota(jnp.int32, (rows, index_row.shape[1]), 0)
    return jnp.where(spots == index_row, 1.0, 0.0).astype(BF16)


def kernel(
    doms, bands, scatter_here, inverse_count,
    type_ref, nodes_ref, shared_ref, v_ref, ham_hbm,
    filt_ref, margin_ref,
    ham, hp, send1, ghost, send2, recv2, send3, recv3, everyone, part, own_part, arrived,
    ham_sem, s1, r1, s2, r2, s3, r3, s4, r4, s5, r5,
):
    dom = lax.axis_index("dom")
    band = lax.axis_index("band")
    nodes, cols = v_ref.shape
    cells, cell_size = nodes_ref.shape
    rim = shared_ref.shape[1] // 2
    slots = nodes + 2 * rim
    present = (dom > 0, dom < doms - 1)
    beside = (jnp.maximum(dom - 1, 0), jnp.minimum(dom + 1, doms - 1))

    load_ham = pltpu.make_async_copy(ham_hbm, ham, ham_sem)
    load_ham.start()

    barrier = pltpu.get_barrier_semaphore()
    for step in range(1, bands):
        pl.semaphore_signal(
            barrier, inc=1,
            device_id={"dom": dom, "band": lax.rem(band + step, bands)},
            device_id_type=MESH,
        )
    if scatter_here:
        for step in range(1, doms):
            pl.semaphore_signal(
                barrier, inc=1,
                device_id={"dom": lax.rem(dom + step, doms), "band": band},
                device_id_type=MESH,
            )
    else:
        for side in (0, 1):
            @pl.when(present[side])
            def _():
                pl.semaphore_signal(
                    barrier, inc=1,
                    device_id={"dom": beside[side], "band": band},
                    device_id_type=MESH,
                )

    for side in (0, 1):
        @pl.when(jnp.logical_not(present[side]))
        def _():
            ghost[side] = jnp.zeros((rim, cols), BF16)
            recv2[side] = jnp.zeros((2, rim, cols), BF16)
            recv3[side] = jnp.zeros((rim, cols), BF16)

    def swap(source, target, sent, got, side, arriving):
        return pltpu.make_async_remote_copy(
            src_ref=source.at[side],
            dst_ref=target.at[side if arriving else 1 - side],
            send_sem=sent.at[side],
            recv_sem=got.at[side if arriving else 1 - side],
            device_id={"dom": beside[side], "band": band},
            device_id_type=MESH,
        )

    def swap_start(*buffers):
        for side in (0, 1):
            @pl.when(present[side])
            def _():
                swap(*buffers, side, False).start()

    def swap_wait(*buffers):
        for side in (0, 1):
            @pl.when(present[side])
            def _():
                swap(*buffers, side, True).wait()

    v = v_ref[...]
    pick = one_hot(nodes, shared_ref[...])
    send1[...] = dot_tn(pick, v).astype(BF16).reshape(2, rim, cols)

    if scatter_here:
        pl.semaphore_wait(barrier, doms - 1 + bands - 1)
    else:
        if bands > 1:
            pl.semaphore_wait(barrier, bands - 1)
        for side in (0, 1):
            @pl.when(present[side])
            def _():
                pl.semaphore_wait(barrier, 1)
    swap_start(send1, ghost, s1, r1)

    load_ham.wait()
    for cell in range(cells):
        slot = nodes_ref[cell : cell + 1, :]
        slot = jnp.where(slot < rim, slot + nodes, jnp.where(slot < nodes + rim, slot - rim, slot))
        spread = one_hot(slots, slot)
        spread_ham = dot(spread, ham[type_ref[cell]]).astype(BF16)
        hp[cell] = dot_nt(spread_ham, spread).astype(BF16)

    def apply(low, high, own, rims):
        total = dot(hp[0, low:high, :nodes], own) + dot(hp[0, low:high, nodes:], rims)
        for cell in range(1, cells):
            total += dot(hp[cell, low:high, :nodes], own) + dot(hp[cell, low:high, nodes:], rims)
        return total

    swap_wait(send1, ghost, s1, r1)
    rims = ghost[...].reshape(2 * rim, cols)
    y_own = apply(0, nodes, v, rims)
    y_rim = apply(nodes, slots, v, rims)
    send2[:, 0] = y_rim.astype(BF16).reshape(2, rim, cols)
    send2[:, 1] = dot_tn(pick, y_own.astype(BF16)).astype(BF16).reshape(2, rim, cols)
    swap_start(send2, recv2, s2, r2)
    v32 = v.astype(F32)
    swap_wait(send2, recv2, s2, r2)
    y_own = y_own + dot(pick, recv2[:, 0].reshape(2 * rim, cols))
    y_rim = y_rim + recv2[:, 1].reshape(2 * rim, cols).astype(F32)
    first = ((y_own - SHIFT * v32) * INV_HALF).astype(BF16)
    first_rim = ((y_rim - SHIFT * rims.astype(F32)) * INV_HALF).reshape(2, rim, cols)
    first_rim = jnp.concatenate(
        [jnp.where(present[side], first_rim[side], 0.0) for side in (0, 1)], axis=0
    ).astype(BF16)

    send3[...] = apply(nodes, slots, first, first_rim).astype(BF16).reshape(2, rim, cols)
    swap_start(send3, recv3, s3, r3)
    second = apply(0, nodes, first, first_rim)
    swap_wait(send3, recv3, s3, r3)
    second = second + dot(pick, recv3[...].reshape(2 * rim, cols))
    filtered = (2.0 * (second - SHIFT * first.astype(F32)) * INV_HALF - v32).astype(BF16)
    filt_ref[...] = filtered

    def share(step):
        return pltpu.make_async_remote_copy(
            src_ref=filt_ref,
            dst_ref=everyone.at[bands - 1 - step],
            send_sem=s4.at[step],
            recv_sem=r4.at[bands - 1 - step],
            device_id={"dom": dom, "band": lax.rem(band + step, bands)},
            device_id_type=MESH,
        )

    for step in range(1, bands):
        share(step).start()

    def give(step, away):
        target = lax.rem(dom + away, doms)
        return pltpu.make_async_remote_copy(
            src_ref=part.at[step, target],
            dst_ref=arrived.at[step, doms - 1 - away],
            send_sem=s5.at[step, away],
            recv_sem=r5.at[step, doms - 1 - away],
            device_id={"dom": target, "band": band},
            device_id_type=MESH,
        )

    for step in range(bands):
        if step == 0:
            other = filtered
        else:
            taken = pltpu.make_async_remote_copy(
                src_ref=filt_ref, dst_ref=everyone.at[step - 1],
                send_sem=s4.at[step], recv_sem=r4.at[step - 1],
                device_id={"dom": dom, "band": lax.rem(band + step, bands)},
                device_id_type=MESH,
            )
            taken.wait_recv()
            other = everyone[step - 1]
        product = dot_tn(filtered, other)
        place = pl.ds(pl.multiple_of(lax.rem(band + step, bands) * cols, 128), cols)
        if scatter_here:
            product = product.reshape(doms, cols // doms, cols)
            part[step] = product.astype(BF16)
            own_part[step] = product
            for away in range(1, doms):
                give(step, away).start()
        else:
            margin_ref[0, :, place] = product

    if scatter_here:
        for step in range(bands):
            total = own_part[step, dom]
            for away in range(1, doms):
                pltpu.make_async_remote_copy(
                    src_ref=part.at[step, dom],
                    dst_ref=arrived.at[step, away - 1],
                    send_sem=s5.at[step, away],
                    recv_sem=r5.at[step, away - 1],
                    device_id={"dom": lax.rem(dom + away, doms), "band": band},
                    device_id_type=MESH,
                ).wait_recv()
                total += arrived[step, away - 1].astype(F32)
            place = pl.ds(pl.multiple_of(lax.rem(band + step, bands) * cols, 128), cols)
            margin_ref[0, :, place] = total * inverse_count
        for step in range(bands):
            for away in range(1, doms):
                give(step, away).wait_send()
    for step in range(1, bands):
        share(step).wait_send()


def solution(mesh):
    doms, bands = mesh.shape["dom"], mesh.shape["band"]

    def on_device(vectors, cell_ham, cell_type, cell_nodes, shared_nodes):
        nodes, cols = vectors.shape
        rim = shared_nodes.shape[1] // 2
        slots = nodes + 2 * rim
        rows = cols // doms
        scatter_here = cols % doms == 0 and rows % 8 == 0
        inverse_count = 1.0 / (nodes * doms)
        kept = (doms, rows) if scatter_here else (1, 8)
        filtered, margin = pl.pallas_call(
            functools.partial(kernel, doms, bands, scatter_here, inverse_count),
            out_shape=(
                jax.ShapeDtypeStruct((nodes, cols), BF16),
                jax.ShapeDtypeStruct((1, rows if scatter_here else cols, bands * cols), F32),
            ),
            in_specs=[pl.BlockSpec(memory_space=pltpu.SMEM)]
            + [pl.BlockSpec(memory_space=pltpu.VMEM)] * 3
            + [pl.BlockSpec(memory_space=pl.ANY)],
            out_specs=(pl.BlockSpec(memory_space=pltpu.VMEM),) * 2,
            scratch_shapes=[
                pltpu.VMEM(cell_ham.shape, BF16),
                pltpu.VMEM((cell_nodes.shape[0], slots, slots), BF16),
                pltpu.VMEM((2, rim, cols), BF16),
                pltpu.VMEM((2, rim, cols), BF16),
                pltpu.VMEM((2, 2, rim, cols), BF16),
                pltpu.VMEM((2, 2, rim, cols), BF16),
                pltpu.VMEM((2, rim, cols), BF16),
                pltpu.VMEM((2, rim, cols), BF16),
                pltpu.VMEM((max(bands - 1, 1), nodes, cols), BF16),
                pltpu.VMEM((bands, *kept, cols), BF16),
                pltpu.VMEM((bands, *kept, cols), F32),
                pltpu.VMEM((bands, *kept, cols), BF16),
                pltpu.SemaphoreType.DMA,
            ]
            + [pltpu.SemaphoreType.DMA((2,))] * 6
            + [pltpu.SemaphoreType.DMA((bands,))] * 2
            + [pltpu.SemaphoreType.DMA((bands, doms if scatter_here else 1))] * 2,
            compiler_params=pltpu.CompilerParams(
                collective_id=0, has_side_effects=True, vmem_limit_bytes=48 << 20
            ),
        )(cell_type, cell_nodes, shared_nodes, vectors, cell_ham)
        if not scatter_here:
            margin = inverse_count * lax.psum_scatter(
                margin, "dom", scatter_dimension=1, tiled=True
            )
        return filtered, margin

    in_specs = (P("dom", "band"), P(), P("dom"), P("dom", None), P("dom", None))
    out_specs = (P("dom", "band"), P("band", "dom", None))
    return jax.shard_map(
        on_device, mesh=mesh, in_specs=in_specs, out_specs=out_specs, check_vma=False
    )
```

```python
import functools

import jax
import jax.numpy as jnp
from jax import lax
from jax.experimental import pallas as pl
from jax.experimental.pallas import tpu as pltpu
from jax.sharding import PartitionSpec as P

SHIFT = 0.5
INV_HALF = 0.5
MESH = pl.DeviceIdType.MESH
F32 = jnp.float32
BF16 = jnp.bfloat16


def dot(a, b):
    return jnp.dot(a, b, preferred_element_type=F32)


def dot_tn(a, b):
    return lax.dot_general(a, b, (((0,), (0,)), ((), ())), preferred_element_type=F32)


def dot_nt(a, b):
    return lax.dot_general(a, b, (((1,), (1,)), ((), ())), preferred_element_type=F32)


def one_hot(rows, index_row):
    spots = lax.broadcasted_iota(jnp.int32, (rows, index_row.shape[1]), 0)
    return jnp.where(spots == index_row, 1.0, 0.0).astype(BF16)


def kernel(
    doms, bands, scatter_here, inverse_count,
    type_hbm, nodes_hbm, shared_hbm, v_hbm, ham_hbm,
    filt_ref, margin_ref,
    type_ref, nodes_ref, shared_ref, v_ref, ham, hp, send1, ghost, send2, recv2, send3, recv3, everyone, part, own_part, arrived,
    in_sem, s1, r1, s2, r2, s3, r3, s4, r4, s5, r5,
):
    dom = lax.axis_index("dom")
    band = lax.axis_index("band")
    nodes, cols = v_ref.shape
    cells, cell_size = nodes_ref.shape
    rim = shared_ref.shape[1] // 2
    slots = nodes + 2 * rim
    present = (dom > 0, dom < doms - 1)
    beside = (jnp.maximum(dom - 1, 0), jnp.minimum(dom + 1, doms - 1))

    load_shared, load_v, load_nodes, load_type, load_ham = [
        pltpu.make_async_copy(source, target, in_sem.at[number])
        for number, (source, target) in enumerate(
            (
                (shared_hbm, shared_ref),
                (v_hbm, v_ref),
                (nodes_hbm, nodes_ref),
                (type_hbm, type_ref),
                (ham_hbm, ham),
            )
        )
    ]
    for load in (load_shared, load_v, load_nodes, load_type, load_ham):
        load.start()

    barrier = pltpu.get_barrier_semaphore()
    for step in range(1, bands):
        pl.semaphore_signal(
            barrier, inc=1,
            device_id={"dom": dom, "band": lax.rem(band + step, bands)},
            device_id_type=MESH,
        )
    if scatter_here:
        for step in range(1, doms):
            pl.semaphore_signal(
                barrier, inc=1,
                device_id={"dom": lax.rem(dom + step, doms), "band": band},
                device_id_type=MESH,
            )
    else:
        for side in (0, 1):
            @pl.when(present[side])
            def _():
                pl.semaphore_signal(
                    barrier, inc=1,
                    device_id={"dom": beside[side], "band": band},
                    device_id_type=MESH,
                )

    for side in (0, 1):
        @pl.when(jnp.logical_not(present[side]))
        def _():
            ghost[side] = jnp.zeros((rim, cols), BF16)
            recv2[side] = jnp.zeros((2, rim, cols), BF16)
            recv3[side] = jnp.zeros((rim, cols), BF16)

    def swap(source, target, sent, got, side, arriving):
        return pltpu.make_async_remote_copy(
            src_ref=source.at[side],
            dst_ref=target.at[side if arriving else 1 - side],
            send_sem=sent.at[side],
            recv_sem=got.at[side if arriving else 1 - side],
            device_id={"dom": beside[side], "band": band},
            device_id_type=MESH,
        )

    def swap_start(*buffers):
        for side in (0, 1):
            @pl.when(present[side])
            def _():
                swap(*buffers, side, False).start()

    def swap_wait(*buffers):
        for side in (0, 1):
            @pl.when(present[side])
            def _():
                swap(*buffers, side, True).wait()

    load_shared.wait()
    load_v.wait()
    v = v_ref[...]
    pick = one_hot(nodes, shared_ref[...])
    send1[...] = dot_tn(pick, v).astype(BF16).reshape(2, rim, cols)

    if scatter_here:
        pl.semaphore_wait(barrier, doms - 1 + bands - 1)
    else:
        if bands > 1:
            pl.semaphore_wait(barrier, bands - 1)
        for side in (0, 1):
            @pl.when(present[side])
            def _():
                pl.semaphore_wait(barrier, 1)
    swap_start(send1, ghost, s1, r1)

    load_nodes.wait()
    load_type.wait()
    load_ham.wait()
    for cell in range(cells):
        slot = nodes_ref[cell : cell + 1, :]
        slot = jnp.where(slot < rim, slot + nodes, jnp.where(slot < nodes + rim, slot - rim, slot))
        spread = one_hot(slots, slot)
        spread_ham = dot(spread, ham[type_ref[cell]]).astype(BF16)
        hp[cell] = dot_nt(spread_ham, spread).astype(BF16)

    def apply(low, high, own, rims):
        total = dot(hp[0, low:high, :nodes], own) + dot(hp[0, low:high, nodes:], rims)
        for cell in range(1, cells):
            total += dot(hp[cell, low:high, :nodes], own) + dot(hp[cell, low:high, nodes:], rims)
        return total

    swap_wait(send1, ghost, s1, r1)
    rims = ghost[...].reshape(2 * rim, cols)
    y_own = apply(0, nodes, v, rims)
    y_rim = apply(nodes, slots, v, rims)
    send2[:, 0] = y_rim.astype(BF16).reshape(2, rim, cols)
    send2[:, 1] = dot_tn(pick, y_own.astype(BF16)).astype(BF16).reshape(2, rim, cols)
    swap_start(send2, recv2, s2, r2)
    v32 = v.astype(F32)
    swap_wait(send2, recv2, s2, r2)
    y_own = y_own + dot(pick, recv2[:, 0].reshape(2 * rim, cols))
    y_rim = y_rim + recv2[:, 1].reshape(2 * rim, cols).astype(F32)
    first = ((y_own - SHIFT * v32) * INV_HALF).astype(BF16)
    first_rim = ((y_rim - SHIFT * rims.astype(F32)) * INV_HALF).reshape(2, rim, cols)
    first_rim = jnp.concatenate(
        [jnp.where(present[side], first_rim[side], 0.0) for side in (0, 1)], axis=0
    ).astype(BF16)

    send3[...] = apply(nodes, slots, first, first_rim).astype(BF16).reshape(2, rim, cols)
    swap_start(send3, recv3, s3, r3)
    second = apply(0, nodes, first, first_rim)
    swap_wait(send3, recv3, s3, r3)
    second = second + dot(pick, recv3[...].reshape(2 * rim, cols))
    filtered = (2.0 * (second - SHIFT * first.astype(F32)) * INV_HALF - v32).astype(BF16)
    filt_ref[...] = filtered

    def share(step):
        return pltpu.make_async_remote_copy(
            src_ref=filt_ref,
            dst_ref=everyone.at[bands - 1 - step],
            send_sem=s4.at[step],
            recv_sem=r4.at[bands - 1 - step],
            device_id={"dom": dom, "band": lax.rem(band + step, bands)},
            device_id_type=MESH,
        )

    for step in range(1, bands):
        share(step).start()

    def give(step, away):
        target = lax.rem(dom + away, doms)
        return pltpu.make_async_remote_copy(
            src_ref=part.at[step, target],
            dst_ref=arrived.at[step, doms - 1 - away],
            send_sem=s5.at[step, away],
            recv_sem=r5.at[step, doms - 1 - away],
            device_id={"dom": target, "band": band},
            device_id_type=MESH,
        )

    for step in range(bands):
        if step == 0:
            other = filtered
        else:
            taken = pltpu.make_async_remote_copy(
                src_ref=filt_ref, dst_ref=everyone.at[step - 1],
                send_sem=s4.at[step], recv_sem=r4.at[step - 1],
                device_id={"dom": dom, "band": lax.rem(band + step, bands)},
                device_id_type=MESH,
            )
            taken.wait_recv()
            other = everyone[step - 1]
        product = dot_tn(filtered, other)
        place = pl.ds(pl.multiple_of(lax.rem(band + step, bands) * cols, 128), cols)
        if scatter_here:
            product = product.reshape(doms, cols // doms, cols)
            part[step] = product.astype(BF16)
            own_part[step] = product
            for away in range(1, doms):
                give(step, away).start()
        else:
            margin_ref[0, :, place] = product

    if scatter_here:
        for step in range(bands):
            total = own_part[step, dom]
            for away in range(1, doms):
                pltpu.make_async_remote_copy(
                    src_ref=part.at[step, dom],
                    dst_ref=arrived.at[step, away - 1],
                    send_sem=s5.at[step, away],
                    recv_sem=r5.at[step, away - 1],
                    device_id={"dom": lax.rem(dom + away, doms), "band": band},
                    device_id_type=MESH,
                ).wait_recv()
                total += arrived[step, away - 1].astype(F32)
            place = pl.ds(pl.multiple_of(lax.rem(band + step, bands) * cols, 128), cols)
            margin_ref[0, :, place] = total * inverse_count
        for step in range(bands):
            for away in range(1, doms):
                give(step, away).wait_send()
    for step in range(1, bands):
        share(step).wait_send()


def solution(mesh):
    doms, bands = mesh.shape["dom"], mesh.shape["band"]

    def on_device(vectors, cell_ham, cell_type, cell_nodes, shared_nodes):
        nodes, cols = vectors.shape
        rim = shared_nodes.shape[1] // 2
        slots = nodes + 2 * rim
        rows = cols // doms
        scatter_here = cols % doms == 0 and rows % 8 == 0
        inverse_count = 1.0 / (nodes * doms)
        kept = (doms, rows) if scatter_here else (1, 8)
        filtered, margin = pl.pallas_call(
            functools.partial(kernel, doms, bands, scatter_here, inverse_count),
            out_shape=(
                jax.ShapeDtypeStruct((nodes, cols), BF16),
                jax.ShapeDtypeStruct((1, rows if scatter_here else cols, bands * cols), F32),
            ),
            in_specs=[pl.BlockSpec(memory_space=pltpu.HBM)] * 5,
            out_specs=(pl.BlockSpec(memory_space=pltpu.VMEM),) * 2,
            scratch_shapes=[
                pltpu.SMEM(cell_type.shape, jnp.int32),
                pltpu.VMEM(cell_nodes.shape, jnp.int32),
                pltpu.VMEM(shared_nodes.shape, jnp.int32),
                pltpu.VMEM(vectors.shape, BF16),
                pltpu.VMEM(cell_ham.shape, BF16),
                pltpu.VMEM((cell_nodes.shape[0], slots, slots), BF16),
                pltpu.VMEM((2, rim, cols), BF16),
                pltpu.VMEM((2, rim, cols), BF16),
                pltpu.VMEM((2, 2, rim, cols), BF16),
                pltpu.VMEM((2, 2, rim, cols), BF16),
                pltpu.VMEM((2, rim, cols), BF16),
                pltpu.VMEM((2, rim, cols), BF16),
                pltpu.VMEM((max(bands - 1, 1), nodes, cols), BF16),
                pltpu.VMEM((bands, *kept, cols), BF16),
                pltpu.VMEM((bands, *kept, cols), F32),
                pltpu.VMEM((bands, *kept, cols), BF16),
                pltpu.SemaphoreType.DMA((5,)),
            ]
            + [pltpu.SemaphoreType.DMA((2,))] * 6
            + [pltpu.SemaphoreType.DMA((bands,))] * 2
            + [pltpu.SemaphoreType.DMA((bands, doms if scatter_here else 1))] * 2,
            compiler_params=pltpu.CompilerParams(
                collective_id=0, has_side_effects=True, vmem_limit_bytes=48 << 20
            ),
        )(cell_type, cell_nodes, shared_nodes, vectors, cell_ham)
        if not scatter_here:
            margin = inverse_count * lax.psum_scatter(
                margin, "dom", scatter_dimension=1, tiled=True
            )
        return filtered, margin

    in_specs = (P("dom", "band"), P(), P("dom"), P("dom", None), P("dom", None))
    out_specs = (P("dom", "band"), P("band", "dom", None))
    return jax.shard_map(
        on_device, mesh=mesh, in_specs=in_specs, out_specs=out_specs, check_vma=False
    )
```

```python
import functools

import jax
import jax.numpy as jnp
from jax import lax
from jax.experimental import pallas as pl
from jax.experimental.pallas import tpu as pltpu
from jax.sharding import PartitionSpec as P

SHIFT = 0.5
INV_HALF = 0.5
GROUP = 4
WIDTHS = (128, 256)
MESH = pl.DeviceIdType.MESH
F32 = jnp.float32
BF16 = jnp.bfloat16


def dot(a, b):
    return jnp.dot(a, b, preferred_element_type=F32)


def dot_tn(a, b):
    return lax.dot_general(a, b, (((0,), (0,)), ((), ())), preferred_element_type=F32)


def dot_nt(a, b):
    return lax.dot_general(a, b, (((1,), (1,)), ((), ())), preferred_element_type=F32)


def one_hot(rows, index_row):
    spots = lax.broadcasted_iota(jnp.int32, (rows, index_row.shape[1]), 0)
    return jnp.where(spots == index_row, 1.0, 0.0).astype(BF16)


def kernel(
    doms, bands, group, chunks, inverse_count,
    type_hbm, nodes_hbm, shared_hbm, v_hbm, ham_hbm,
    filt_ref, margin_ref,
    type_ref, nodes_ref, shared_ref, v_ref, ham, hp,
    send1, ghost, send2, recv2, send3, recv3, everyone,
    part, own_part, arrived, part2, own_part2, arrived2,
    in_sem, s1, r1, s2, r2, s3, r3, s4, r4, s5, r5, s6, r6,
):
    dom = lax.axis_index("dom")
    band = lax.axis_index("band")
    nodes, cols = v_ref.shape
    cells = nodes_ref.shape[0]
    rim = shared_ref.shape[1] // 2
    slots = nodes + 2 * rim
    groups = doms // group if group else 0
    present = (dom > 0, dom < doms - 1)
    beside = (jnp.maximum(dom - 1, 0), jnp.minimum(dom + 1, doms - 1))

    load_shared, load_v, load_nodes, load_type, load_ham = [
        pltpu.make_async_copy(source, target, in_sem.at[number])
        for number, (source, target) in enumerate(
            (
                (shared_hbm, shared_ref),
                (v_hbm, v_ref),
                (nodes_hbm, nodes_ref),
                (type_hbm, type_ref),
                (ham_hbm, ham),
            )
        )
    ]

    barrier = pltpu.get_barrier_semaphore()

    def greet(other_dom, other_band):
        pl.semaphore_signal(
            barrier, inc=1,
            device_id={"dom": other_dom, "band": other_band},
            device_id_type=MESH,
        )

    if group:
        inside, stack = lax.rem(dom, group), dom // group
        mates = [stack * group + lax.rem(inside + away, group) for away in range(1, group)]
        tower = [lax.rem(stack + away, groups) * group + inside for away in range(1, groups)]
        lonely = (
            jnp.logical_and(present[0], inside == 0),
            jnp.logical_and(present[1], inside == group - 1),
        )
    else:
        mates, tower, lonely = [], [], present
    for side in (0, 1):
        @pl.when(lonely[side])
        def _():
            greet(beside[side], band)
    for mate in mates + tower:
        greet(mate, band)
    for step in range(1, bands):
        greet(dom, lax.rem(band + step, bands))
    for load in (load_shared, load_v, load_nodes, load_type, load_ham):
        load.start()

    for side in (0, 1):
        @pl.when(jnp.logical_not(present[side]))
        def _():
            ghost[side] = jnp.zeros((rim, cols), BF16)
            recv2[side] = jnp.zeros((2, rim, cols), BF16)
            recv3[side] = jnp.zeros((rim, cols), BF16)

    def swap(source, target, sent, got, chunk, side, arriving):
        low, high = chunks[chunk]
        landing = side if arriving else 1 - side
        return pltpu.make_async_remote_copy(
            src_ref=source.at[side, ..., low:high],
            dst_ref=target.at[landing, ..., low:high],
            send_sem=sent.at[chunk, side],
            recv_sem=got.at[chunk, landing],
            device_id={"dom": beside[side], "band": band},
            device_id_type=MESH,
        )

    def swap_start(*args):
        for side in (0, 1):
            @pl.when(present[side])
            def _():
                swap(*args, side, False).start()

    def swap_wait(*args):
        for side in (0, 1):
            @pl.when(present[side])
            def _():
                swap(*args, side, True).wait()

    load_shared.wait()
    load_v.wait()
    pick = one_hot(nodes, shared_ref[...])
    send1[...] = dot_tn(pick, v_ref[...]).astype(BF16).reshape(2, rim, cols)

    fixed = len(mates) + len(tower) + bands - 1
    pl.semaphore_wait(
        barrier, fixed + jnp.where(lonely[0], 1, 0) + jnp.where(lonely[1], 1, 0)
    )
    numbers = range(len(chunks))
    for chunk in numbers:
        swap_start(send1, ghost, s1, r1, chunk)

    load_nodes.wait()
    load_type.wait()
    load_ham.wait()
    for cell in range(cells):
        slot = nodes_ref[cell : cell + 1, :]
        slot = jnp.where(slot < rim, slot + nodes, jnp.where(slot < nodes + rim, slot - rim, slot))
        spread = one_hot(slots, slot)
        spread_ham = dot(spread, ham[type_ref[cell]]).astype(BF16)
        hp[cell] = dot_nt(spread_ham, spread).astype(BF16)

    def apply(low, high, own, rims):
        total = dot(hp[0, low:high, :nodes], own) + dot(hp[0, low:high, nodes:], rims)
        for cell in range(1, cells):
            total += dot(hp[cell, low:high, :nodes], own) + dot(hp[cell, low:high, nodes:], rims)
        return total

    held = []
    for chunk, (low, high) in enumerate(chunks):
        wide = high - low
        swap_wait(send1, ghost, s1, r1, chunk)
        v = v_ref[:, low:high]
        rims = ghost[:, :, low:high].reshape(2 * rim, wide)
        y_own = apply(0, nodes, v, rims)
        send2[:, 1, :, low:high] = (
            dot_tn(pick, y_own.astype(BF16)).astype(BF16).reshape(2, rim, wide)
        )
        y_rim = apply(nodes, slots, v, rims)
        send2[:, 0, :, low:high] = y_rim.astype(BF16).reshape(2, rim, wide)
        swap_start(send2, recv2, s2, r2, chunk)
        held.append((y_own, y_rim))

    again = []
    for chunk, (low, high) in enumerate(chunks):
        wide = high - low
        y_own, y_rim = held[chunk]
        v32 = v_ref[:, low:high].astype(F32)
        rims = ghost[:, :, low:high].reshape(2 * rim, wide).astype(F32)
        swap_wait(send2, recv2, s2, r2, chunk)
        y_own = y_own + dot(pick, recv2[:, 0, :, low:high].reshape(2 * rim, wide))
        y_rim = y_rim + recv2[:, 1, :, low:high].reshape(2 * rim, wide).astype(F32)
        first = ((y_own - SHIFT * v32) * INV_HALF).astype(BF16)
        first_rim = ((y_rim - SHIFT * rims) * INV_HALF).reshape(2, rim, wide)
        first_rim = jnp.concatenate(
            [jnp.where(present[side], first_rim[side], 0.0) for side in (0, 1)], axis=0
        ).astype(BF16)
        out_rim = apply(nodes, slots, first, first_rim)
        send3[:, :, low:high] = out_rim.astype(BF16).reshape(2, rim, wide)
        swap_start(send3, recv3, s3, r3, chunk)
        again.append((apply(0, nodes, first, first_rim), first))

    def share(chunk, step, arriving=False):
        low, high = chunks[chunk]
        landing = step - 1 if arriving else bands - 1 - step
        return pltpu.make_async_remote_copy(
            src_ref=filt_ref.at[:, low:high],
            dst_ref=everyone.at[landing, :, low:high],
            send_sem=s4.at[chunk, step],
            recv_sem=r4.at[chunk, landing],
            device_id={"dom": dom, "band": lax.rem(band + step, bands)},
            device_id_type=MESH,
        )

    for chunk, (low, high) in enumerate(chunks):
        wide = high - low
        second, first = again[chunk]
        v32 = v_ref[:, low:high].astype(F32)
        swap_wait(send3, recv3, s3, r3, chunk)
        second = second + dot(pick, recv3[:, :, low:high].reshape(2 * rim, wide))
        filt_ref[:, low:high] = (
            2.0 * (second - SHIFT * first.astype(F32)) * INV_HALF - v32
        ).astype(BF16)
        for step in range(1, bands):
            share(chunk, step).start()

    def give(step, away, arriving=False):
        landing = away - 1 if arriving else group - 1 - away
        target = lax.rem(inside + away, group)
        return pltpu.make_async_remote_copy(
            src_ref=part.at[step, target],
            dst_ref=arrived.at[step, landing],
            send_sem=s5.at[step, away],
            recv_sem=r5.at[step, landing],
            device_id={"dom": stack * group + target, "band": band},
            device_id_type=MESH,
        )

    def climb(step, away, arriving=False):
        landing = away - 1 if arriving else groups - 1 - away
        target = lax.rem(stack + away, groups)
        return pltpu.make_async_remote_copy(
            src_ref=part2.at[step, target],
            dst_ref=arrived2.at[step, landing],
            send_sem=s6.at[step, away],
            recv_sem=r6.at[step, landing],
            device_id={"dom": target * group + inside, "band": band},
            device_id_type=MESH,
        )

    def place(step):
        return pl.ds(pl.multiple_of(lax.rem(band + step, bands) * cols, 128), cols)

    for step in range(bands):
        if step == 0:
            other = filt_ref[...]
        else:
            for chunk in numbers:
                share(chunk, step, True).wait_recv()
            other = everyone[step - 1]
        product = dot_tn(filt_ref[...], other)
        if not group:
            margin_ref[0, :, place(step)] = product
            continue
        rows = cols // doms
        for member in range(group):
            block = jnp.concatenate(
                [
                    product[(layer * group + member) * rows : (layer * group + member + 1) * rows]
                    for layer in range(groups)
                ],
                axis=0,
            )
            own_part[step, member] = block
            part[step, member] = block.astype(BF16)
        for away in range(1, group):
            give(step, away).start()

    if group:
        for step in range(bands):
            total = own_part[step, inside]
            for away in range(1, group):
                give(step, away, True).wait_recv()
                total += arrived[step, away - 1].astype(F32)
            for layer in range(groups):
                block = total[layer * rows : (layer + 1) * rows]
                own_part2[step, layer] = block
                part2[step, layer] = block.astype(BF16)
            for away in range(1, groups):
                climb(step, away).start()
        for step in range(bands):
            total = own_part2[step, stack]
            for away in range(1, groups):
                climb(step, away, True).wait_recv()
                total += arrived2[step, away - 1].astype(F32)
            margin_ref[0, :, place(step)] = total * inverse_count
        for step in range(bands):
            for away in range(1, group):
                give(step, away).wait_send()
            for away in range(1, groups):
                climb(step, away).wait_send()
    for chunk in numbers:
        for step in range(1, bands):
            share(chunk, step).wait_send()


def solution(mesh):
    doms, bands = mesh.shape["dom"], mesh.shape["band"]

    def on_device(vectors, cell_ham, cell_type, cell_nodes, shared_nodes):
        nodes, cols = vectors.shape
        rim = shared_nodes.shape[1] // 2
        slots = nodes + 2 * rim
        rows = cols // doms
        scatter_here = cols % doms == 0 and rows % 8 == 0 and doms % GROUP == 0 and doms > GROUP
        group = GROUP if scatter_here else 0
        groups = doms // GROUP
        inverse_count = 1.0 / (nodes * doms)
        chunks = []
        for width in WIDTHS + (cols,):
            low = chunks[-1][1] if chunks else 0
            if low < cols:
                chunks.append((low, min(low + width, cols)))
        if scatter_here:
            kept = [
                pltpu.VMEM((bands, group, groups * rows, cols), BF16),
                pltpu.VMEM((bands, group, groups * rows, cols), F32),
                pltpu.VMEM((bands, group - 1, groups * rows, cols), BF16),
                pltpu.VMEM((bands, groups, rows, cols), BF16),
                pltpu.VMEM((bands, groups, rows, cols), F32),
                pltpu.VMEM((bands, groups - 1, rows, cols), BF16),
            ]
        else:
            kept = [pltpu.VMEM((8, 128), F32)] * 6
        operands = [
            pltpu.with_memory_space_constraint(operand, pltpu.HBM)
            for operand in (cell_type, cell_nodes, shared_nodes, vectors, cell_ham)
        ]
        filtered, margin = pl.pallas_call(
            functools.partial(kernel, doms, bands, group, tuple(chunks), inverse_count),
            out_shape=(
                jax.ShapeDtypeStruct((nodes, cols), BF16),
                jax.ShapeDtypeStruct((1, rows if scatter_here else cols, bands * cols), F32),
            ),
            in_specs=[pl.BlockSpec(memory_space=pltpu.HBM)] * 5,
            out_specs=(pl.BlockSpec(memory_space=pltpu.VMEM),) * 2,
            scratch_shapes=[
                pltpu.SMEM(cell_type.shape, jnp.int32),
                pltpu.VMEM(cell_nodes.shape, jnp.int32),
                pltpu.VMEM(shared_nodes.shape, jnp.int32),
                pltpu.VMEM(vectors.shape, BF16),
                pltpu.VMEM(cell_ham.shape, BF16),
                pltpu.VMEM((cell_nodes.shape[0], slots, slots), BF16),
                pltpu.VMEM((2, rim, cols), BF16),
                pltpu.VMEM((2, rim, cols), BF16),
                pltpu.VMEM((2, 2, rim, cols), BF16),
                pltpu.VMEM((2, 2, rim, cols), BF16),
                pltpu.VMEM((2, rim, cols), BF16),
                pltpu.VMEM((2, rim, cols), BF16),
                pltpu.VMEM((max(bands - 1, 1), nodes, cols), BF16),
            ]
            + kept
            + [pltpu.SemaphoreType.DMA((5,))]
            + [pltpu.SemaphoreType.DMA((len(chunks), 2))] * 6
            + [pltpu.SemaphoreType.DMA((len(chunks), bands))] * 2
            + [pltpu.SemaphoreType.DMA((bands, GROUP))] * 2
            + [pltpu.SemaphoreType.DMA((bands, groups if scatter_here else 1))] * 2,
            compiler_params=pltpu.CompilerParams(
                collective_id=0, has_side_effects=True, vmem_limit_bytes=48 << 20
            ),
        )(*operands)
        if not scatter_here:
            margin = inverse_count * lax.psum_scatter(
                margin, "dom", scatter_dimension=1, tiled=True
            )
        return filtered, margin

    in_specs = (P("dom", "band"), P(), P("dom"), P("dom", None), P("dom", None))
    out_specs = (P("dom", "band"), P("band", "dom", None))
    return jax.shard_map(
        on_device, mesh=mesh, in_specs=in_specs, out_specs=out_specs, check_vma=False
    )
```

```python
import functools

import jax
import jax.numpy as jnp
from jax import lax
from jax.experimental import pallas as pl
from jax.experimental.pallas import tpu as pltpu
from jax.sharding import PartitionSpec as P

SHIFT = 0.5
INV_HALF = 0.5
GROUP = 4
WIDTHS = (128, 128, 128)
MESH = pl.DeviceIdType.MESH
F32 = jnp.float32
BF16 = jnp.bfloat16


def dot(a, b):
    return jnp.dot(a, b, preferred_element_type=F32)


def dot_tn(a, b):
    return lax.dot_general(a, b, (((0,), (0,)), ((), ())), preferred_element_type=F32)


def dot_nt(a, b):
    return lax.dot_general(a, b, (((1,), (1,)), ((), ())), preferred_element_type=F32)


def one_hot(rows, index_row):
    spots = lax.broadcasted_iota(jnp.int32, (rows, index_row.shape[1]), 0)
    return jnp.where(spots == index_row, 1.0, 0.0).astype(BF16)


def kernel(
    doms, bands, group, chunks, inverse_count,
    type_hbm, nodes_hbm, shared_hbm, v_hbm, ham_hbm,
    filt_ref, margin_ref,
    type_ref, nodes_ref, shared_ref, v_ref, ham, hp,
    send1, ghost, send2, recv2, send3, recv3, everyone,
    part, own_part, arrived, part2, own_part2, arrived2,
    in_sem, s1, r1, s2, r2, s3, r3, s4, r4, s5, r5, s6, r6,
):
    dom = lax.axis_index("dom")
    band = lax.axis_index("band")
    nodes, cols = v_ref.shape
    cells = nodes_ref.shape[0]
    rim = shared_ref.shape[1] // 2
    slots = nodes + 2 * rim
    groups = doms // group if group else 0
    present = (dom > 0, dom < doms - 1)
    beside = (jnp.maximum(dom - 1, 0), jnp.minimum(dom + 1, doms - 1))

    load_shared, load_v, load_nodes, load_type, load_ham = [
        pltpu.make_async_copy(source, target, in_sem.at[number])
        for number, (source, target) in enumerate(
            (
                (shared_hbm, shared_ref),
                (v_hbm, v_ref),
                (nodes_hbm, nodes_ref),
                (type_hbm, type_ref),
                (ham_hbm, ham),
            )
        )
    ]

    barrier = pltpu.get_barrier_semaphore()

    def greet(other_dom, other_band):
        pl.semaphore_signal(
            barrier, inc=1,
            device_id={"dom": other_dom, "band": other_band},
            device_id_type=MESH,
        )

    if group:
        inside, stack = lax.rem(dom, group), dom // group
        mates = [stack * group + lax.rem(inside + away, group) for away in range(1, group)]
        tower = [lax.rem(stack + away, groups) * group + inside for away in range(1, groups)]
        lonely = (
            jnp.logical_and(present[0], inside == 0),
            jnp.logical_and(present[1], inside == group - 1),
        )
    else:
        mates, tower, lonely = [], [], present
    for side in (0, 1):
        @pl.when(lonely[side])
        def _():
            greet(beside[side], band)
    for mate in mates + tower:
        greet(mate, band)
    for step in range(1, bands):
        greet(dom, lax.rem(band + step, bands))
    for load in (load_shared, load_v, load_nodes, load_type, load_ham):
        load.start()

    for side in (0, 1):
        @pl.when(jnp.logical_not(present[side]))
        def _():
            ghost[side] = jnp.zeros((rim, cols), BF16)
            recv2[side] = jnp.zeros((2, rim, cols), BF16)
            recv3[side] = jnp.zeros((rim, cols), BF16)

    def swap(source, target, sent, got, chunk, side, arriving):
        low, high = chunks[chunk]
        landing = side if arriving else 1 - side
        return pltpu.make_async_remote_copy(
            src_ref=source.at[side, ..., low:high],
            dst_ref=target.at[landing, ..., low:high],
            send_sem=sent.at[chunk, side],
            recv_sem=got.at[chunk, landing],
            device_id={"dom": beside[side], "band": band},
            device_id_type=MESH,
        )

    def swap_start(*args):
        for side in (0, 1):
            @pl.when(present[side])
            def _():
                swap(*args, side, False).start()

    def swap_wait(*args):
        for side in (0, 1):
            @pl.when(present[side])
            def _():
                swap(*args, side, True).wait()

    load_shared.wait()
    load_v.wait()
    pick = one_hot(nodes, shared_ref[...])
    send1[...] = dot_tn(pick, v_ref[...]).astype(BF16).reshape(2, rim, cols)

    fixed = len(mates) + len(tower) + bands - 1
    pl.semaphore_wait(
        barrier, fixed + jnp.where(lonely[0], 1, 0) + jnp.where(lonely[1], 1, 0)
    )
    numbers = range(len(chunks))
    for chunk in numbers:
        swap_start(send1, ghost, s1, r1, chunk)

    load_nodes.wait()
    load_type.wait()
    load_ham.wait()
    for cell in range(cells):
        slot = nodes_ref[cell : cell + 1, :]
        slot = jnp.where(slot < rim, slot + nodes, jnp.where(slot < nodes + rim, slot - rim, slot))
        spread = one_hot(slots, slot)
        spread_ham = dot(spread, ham[type_ref[cell]]).astype(BF16)
        hp[cell] = dot_nt(spread_ham, spread).astype(BF16)

    def apply(low, high, own, rims):
        total = dot(hp[0, low:high, :nodes], own) + dot(hp[0, low:high, nodes:], rims)
        for cell in range(1, cells):
            total += dot(hp[cell, low:high, :nodes], own) + dot(hp[cell, low:high, nodes:], rims)
        return total

    held = []
    for chunk, (low, high) in enumerate(chunks):
        wide = high - low
        swap_wait(send1, ghost, s1, r1, chunk)
        v = v_ref[:, low:high]
        rims = ghost[:, :, low:high].reshape(2 * rim, wide)
        y_own = apply(0, nodes, v, rims)
        send2[:, 1, :, low:high] = (
            dot_tn(pick, y_own.astype(BF16)).astype(BF16).reshape(2, rim, wide)
        )
        y_rim = apply(nodes, slots, v, rims)
        send2[:, 0, :, low:high] = y_rim.astype(BF16).reshape(2, rim, wide)
        swap_start(send2, recv2, s2, r2, chunk)
        held.append((y_own, y_rim))

    again = []
    for chunk, (low, high) in enumerate(chunks):
        wide = high - low
        y_own, y_rim = held[chunk]
        v32 = v_ref[:, low:high].astype(F32)
        rims = ghost[:, :, low:high].reshape(2 * rim, wide).astype(F32)
        swap_wait(send2, recv2, s2, r2, chunk)
        y_own = y_own + dot(pick, recv2[:, 0, :, low:high].reshape(2 * rim, wide))
        y_rim = y_rim + recv2[:, 1, :, low:high].reshape(2 * rim, wide).astype(F32)
        first = ((y_own - SHIFT * v32) * INV_HALF).astype(BF16)
        first_rim = ((y_rim - SHIFT * rims) * INV_HALF).reshape(2, rim, wide)
        first_rim = jnp.concatenate(
            [jnp.where(present[side], first_rim[side], 0.0) for side in (0, 1)], axis=0
        ).astype(BF16)
        out_rim = apply(nodes, slots, first, first_rim)
        send3[:, :, low:high] = out_rim.astype(BF16).reshape(2, rim, wide)
        swap_start(send3, recv3, s3, r3, chunk)
        again.append((apply(0, nodes, first, first_rim), first))

    def share(chunk, step, arriving=False):
        low, high = chunks[chunk]
        landing = step - 1 if arriving else bands - 1 - step
        return pltpu.make_async_remote_copy(
            src_ref=filt_ref.at[:, low:high],
            dst_ref=everyone.at[landing, :, low:high],
            send_sem=s4.at[chunk, step],
            recv_sem=r4.at[chunk, landing],
            device_id={"dom": dom, "band": lax.rem(band + step, bands)},
            device_id_type=MESH,
        )

    for chunk, (low, high) in enumerate(chunks):
        wide = high - low
        second, first = again[chunk]
        v32 = v_ref[:, low:high].astype(F32)
        swap_wait(send3, recv3, s3, r3, chunk)
        second = second + dot(pick, recv3[:, :, low:high].reshape(2 * rim, wide))
        filt_ref[:, low:high] = (
            2.0 * (second - SHIFT * first.astype(F32)) * INV_HALF - v32
        ).astype(BF16)
        for step in range(1, bands):
            share(chunk, step).start()

    def give(step, away, arriving=False):
        landing = away - 1 if arriving else group - 1 - away
        target = lax.rem(inside + away, group)
        return pltpu.make_async_remote_copy(
            src_ref=part.at[step, target],
            dst_ref=arrived.at[step, landing],
            send_sem=s5.at[step, away],
            recv_sem=r5.at[step, landing],
            device_id={"dom": stack * group + target, "band": band},
            device_id_type=MESH,
        )

    def climb(step, away, arriving=False):
        landing = away - 1 if arriving else groups - 1 - away
        target = lax.rem(stack + away, groups)
        return pltpu.make_async_remote_copy(
            src_ref=part2.at[step, target],
            dst_ref=arrived2.at[step, landing],
            send_sem=s6.at[step, away],
            recv_sem=r6.at[step, landing],
            device_id={"dom": target * group + inside, "band": band},
            device_id_type=MESH,
        )

    def place(step):
        return pl.ds(pl.multiple_of(lax.rem(band + step, bands) * cols, 128), cols)

    for step in range(bands):
        if step == 0:
            other = filt_ref[...]
        else:
            for chunk in numbers:
                share(chunk, step, True).wait_recv()
            other = everyone[step - 1]
        product = dot_tn(filt_ref[...], other)
        if not group:
            margin_ref[0, :, place(step)] = product
            continue
        rows = cols // doms
        for member in range(group):
            block = jnp.concatenate(
                [
                    product[(layer * group + member) * rows : (layer * group + member + 1) * rows]
                    for layer in range(groups)
                ],
                axis=0,
            )
            own_part[step, member] = block
            part[step, member] = block.astype(BF16)
        for away in range(1, group):
            give(step, away).start()

    if group:
        for step in range(bands):
            total = own_part[step, inside]
            for away in range(1, group):
                give(step, away, True).wait_recv()
                total += arrived[step, away - 1].astype(F32)
            for layer in range(groups):
                block = total[layer * rows : (layer + 1) * rows]
                own_part2[step, layer] = block
                part2[step, layer] = block.astype(BF16)
            for away in range(1, groups):
                climb(step, away).start()
        for step in range(bands):
            total = own_part2[step, stack]
            for away in range(1, groups):
                climb(step, away, True).wait_recv()
                total += arrived2[step, away - 1].astype(F32)
            margin_ref[0, :, place(step)] = total * inverse_count
        for step in range(bands):
            for away in range(1, group):
                give(step, away).wait_send()
            for away in range(1, groups):
                climb(step, away).wait_send()
    for chunk in numbers:
        for step in range(1, bands):
            share(chunk, step).wait_send()


def solution(mesh):
    doms, bands = mesh.shape["dom"], mesh.shape["band"]

    def on_device(vectors, cell_ham, cell_type, cell_nodes, shared_nodes):
        nodes, cols = vectors.shape
        rim = shared_nodes.shape[1] // 2
        slots = nodes + 2 * rim
        rows = cols // doms
        scatter_here = cols % doms == 0 and rows % 8 == 0 and doms % GROUP == 0 and doms > GROUP
        group = GROUP if scatter_here else 0
        groups = doms // GROUP
        inverse_count = 1.0 / (nodes * doms)
        chunks = []
        for width in WIDTHS + (cols,):
            low = chunks[-1][1] if chunks else 0
            if low < cols:
                chunks.append((low, min(low + width, cols)))
        if scatter_here:
            kept = [
                pltpu.VMEM((bands, group, groups * rows, cols), BF16),
                pltpu.VMEM((bands, group, groups * rows, cols), F32),
                pltpu.VMEM((bands, group - 1, groups * rows, cols), BF16),
                pltpu.VMEM((bands, groups, rows, cols), BF16),
                pltpu.VMEM((bands, groups, rows, cols), F32),
                pltpu.VMEM((bands, groups - 1, rows, cols), BF16),
            ]
        else:
            kept = [pltpu.VMEM((8, 128), F32)] * 6
        operands = [
            pltpu.with_memory_space_constraint(operand, pltpu.HBM)
            for operand in (cell_type, cell_nodes, shared_nodes, vectors, cell_ham)
        ]
        filtered, margin = pl.pallas_call(
            functools.partial(kernel, doms, bands, group, tuple(chunks), inverse_count),
            out_shape=(
                jax.ShapeDtypeStruct((nodes, cols), BF16),
                jax.ShapeDtypeStruct((1, rows if scatter_here else cols, bands * cols), F32),
            ),
            in_specs=[pl.BlockSpec(memory_space=pltpu.HBM)] * 5,
            out_specs=(pl.BlockSpec(memory_space=pltpu.VMEM),) * 2,
            scratch_shapes=[
                pltpu.SMEM(cell_type.shape, jnp.int32),
                pltpu.VMEM(cell_nodes.shape, jnp.int32),
                pltpu.VMEM(shared_nodes.shape, jnp.int32),
                pltpu.VMEM(vectors.shape, BF16),
                pltpu.VMEM(cell_ham.shape, BF16),
                pltpu.VMEM((cell_nodes.shape[0], slots, slots), BF16),
                pltpu.VMEM((2, rim, cols), BF16),
                pltpu.VMEM((2, rim, cols), BF16),
                pltpu.VMEM((2, 2, rim, cols), BF16),
                pltpu.VMEM((2, 2, rim, cols), BF16),
                pltpu.VMEM((2, rim, cols), BF16),
                pltpu.VMEM((2, rim, cols), BF16),
                pltpu.VMEM((max(bands - 1, 1), nodes, cols), BF16),
            ]
            + kept
            + [pltpu.SemaphoreType.DMA((5,))]
            + [pltpu.SemaphoreType.DMA((len(chunks), 2))] * 6
            + [pltpu.SemaphoreType.DMA((len(chunks), bands))] * 2
            + [pltpu.SemaphoreType.DMA((bands, GROUP))] * 2
            + [pltpu.SemaphoreType.DMA((bands, groups if scatter_here else 1))] * 2,
            compiler_params=pltpu.CompilerParams(
                collective_id=0, has_side_effects=True, vmem_limit_bytes=48 << 20
            ),
        )(*operands)
        if not scatter_here:
            margin = inverse_count * lax.psum_scatter(
                margin, "dom", scatter_dimension=1, tiled=True
            )
        return filtered, margin

    in_specs = (P("dom", "band"), P(), P("dom"), P("dom", None), P("dom", None))
    out_specs = (P("dom", "band"), P("band", "dom", None))
    return jax.shard_map(
        on_device, mesh=mesh, in_specs=in_specs, out_specs=out_specs, check_vma=False
    )
```
